32 devices in a mesh: groups: 2 (over x), seq: 8 (over z, y), head: 2 (over core).
Axes of the slice: x: 2, y: 2, z: 4, core: 2. Of those that a mesh axis runs over, the one named last changes fastest.
Arguments:
- queries: bfloat16 [512, 4096], P(('groups', 'seq'), 'head'), parts along dimension 0, may hold values from -24 to 24
- vision: bfloat16 [4096, 7680], P(('groups', 'seq')), parts along dimension 0, may hold values from -6 to 6
- key_matrix: bfloat16 [7680, 512], P('seq', 'head'), may hold values from -0.0625 to 0.0625
- value_matrix: bfloat16 [7680, 512], P('seq', 'head'), may hold values from -0.0625 to 0.0625
- out_weight: bfloat16 [4096, 8192], P('head', 'seq'), may hold values from -0.09375 to 0.09375
- residual: bfloat16 [512, 8192], P(('groups', 'head'), 'seq'), parts along dimension 0, may hold values from -4 to 4
- query_norm_gain: float32 [128], replicated, may hold values from 1 to 12
- key_norm_gain: float32 [128], replicated, may hold values from 1 to 12
- attn_gate: float32 [1], replicated, may hold values from 0.5 to 2
Outputs:
- mixed: bfloat16 [512, 8192], P(('groups', 'head'), 'seq'), parts along dimension 0
The draws below stay inside these ranges and needn't reach their ends.
There are 2 independent parts, one for each index of `groups`. The reference program is written for one: setup_inputs(seed, part) draws one part's arguments, and reference() takes and returns one part's arrays. A program takes and returns all parts, laid end to end along the dimension named above; an argument that names none is the same for every part. Nothing has to cross between parts.
All inputs are finite; a program needn't handle non-finite values.
Results may differ from the reference program's by a relative error of at most 0.015.
The reference program's roundings to bfloat16 on the way count: a program that leaves them out, or rounds other values in their place, can miss the bound.
Values may be sent and summed in bfloat16 or wider, within the bound.
A program may use at most 64 MiB of HBM per device.

```python
import math
import jax
import jax.numpy as jnp
from jax import lax

D = 8192
VISION_WIDTH = 7680
HEAD_SIZE = 128
QUERY_HEADS = 32
KEY_VALUE_HEADS = 4
TEXT_TOKENS = 256
VISION_TOKENS = 2048


def draw_queries(key, part):
    base = jax.random.normal(key, (TEXT_TOKENS, QUERY_HEADS * HEAD_SIZE), jnp.float32)
    return jnp.clip(base, -6.0, 6.0).astype(jnp.bfloat16)


def gain_values(key, salt):
    base = jnp.exp(jax.random.uniform(jax.random.fold_in(key, salt), (HEAD_SIZE,), jnp.float32, 0.0, math.log(3.0)))
    return base


def draw_query_norm_gain(key, part):
    return gain_values(key, 21)


def draw_key_norm_gain(key, part):
    return gain_values(key, 37)


def steps_of(stream_key, dims, cuts, low, largest):
    level, own = 1.0, jax.random.fold_in(stream_key, 6)
    for dim, blocks in cuts:
        draws = jnp.exp(jax.random.uniform(jax.random.fold_in(own, dim), (blocks,), jnp.float32, low / len(cuts), largest / len(cuts)))
        level = level * jnp.repeat(draws, dims[dim] // blocks).reshape([-1 if axis == dim else 1 for axis in range(len(dims))])
    return level


def noise(rng, extent, deviation, most, shards=(), dtype=jnp.bfloat16):
    loudness = steps_of(rng, extent, shards, -0.22, 0.18) if shards else 1.0
    result = jax.random.normal(rng, extent, jnp.float32) * deviation * loudness
    return jnp.minimum(jnp.maximum(result, -most), most).astype(dtype)


def setup_inputs(seed: int = 0, part: int = 0) -> dict:
    key_list = jax.random.split(jax.random.key(seed), 10)
    own_keys = jax.random.split(jax.random.fold_in(key_list[9], part), 10)
    return {
        "queries": draw_queries(jax.random.fold_in(jax.random.fold_in(key_list[9], part), 71), part),
        "vision": noise(own_keys[1], (VISION_TOKENS, VISION_WIDTH), 1.0, 6.0, ((0, 8),)),
        "key_matrix": noise(key_list[2], (VISION_WIDTH, KEY_VALUE_HEADS * HEAD_SIZE), VISION_WIDTH ** -0.5, 0.0625, ((0, 8), (1, 2))),
        "value_matrix": noise(key_list[3], (VISION_WIDTH, KEY_VALUE_HEADS * HEAD_SIZE), VISION_WIDTH ** -0.5, 0.0625, ((0, 8), (1, 2))),
        "out_weight": noise(key_list[4], (QUERY_HEADS * HEAD_SIZE, D), (QUERY_HEADS * HEAD_SIZE) ** -0.5, 0.09375, ((0, 2), (1, 8))),
        "residual": noise(own_keys[5], (TEXT_TOKENS, D), 0.3, 4.0, ((0, 2), (1, 8))),
        "query_norm_gain": draw_query_norm_gain(jax.random.fold_in(key_list[9], 71), part),
        "key_norm_gain": draw_key_norm_gain(jax.random.fold_in(key_list[9], 71), part),
        "attn_gate": jnp.clip(jax.random.uniform(key_list[8], (1,), jnp.float32, 0.5, 2.0), 0.5, 2.0),
    }


epsilon = 1e-05

def apply_norm(value_heads, gain):
    return value_heads * lax.rsqrt(lax.optimization_barrier(jnp.mean(value_heads * value_heads, axis=-1, keepdims=True)) + epsilon) * gain

def reference(queries, vision, key_matrix, value_matrix, out_weight, residual, query_norm_gain, key_norm_gain, attn_gate):
    expanded_keys = jnp.dot(vision, key_matrix, preferred_element_type=jnp.float32)
    expanded_values = jnp.dot(vision, value_matrix, preferred_element_type=jnp.float32)
    key_heads = apply_norm(expanded_keys.reshape(VISION_TOKENS, KEY_VALUE_HEADS, HEAD_SIZE), key_norm_gain).astype(jnp.bfloat16)
    value_heads = expanded_values.reshape(VISION_TOKENS, KEY_VALUE_HEADS, HEAD_SIZE).astype(jnp.bfloat16)
    heads_per_group = QUERY_HEADS // KEY_VALUE_HEADS
    norm_result = apply_norm(queries.astype(jnp.float32).reshape(TEXT_TOKENS, KEY_VALUE_HEADS, heads_per_group, HEAD_SIZE), query_norm_gain).astype(jnp.bfloat16)
    rows_per_block = 128 if TEXT_TOKENS % 128 == 0 else TEXT_TOKENS
    blocked_queries = norm_result.reshape(TEXT_TOKENS // rows_per_block, rows_per_block, KEY_VALUE_HEADS, heads_per_group, HEAD_SIZE)
    keys_wide = key_heads.astype(jnp.float32)
    values_wide = value_heads.astype(jnp.float32)

    def attend_block(query_block):
        scores = jnp.einsum('tgqd,rgd->tgqr', query_block.astype(jnp.float32), keys_wide) * HEAD_SIZE ** (-0.5)
        maxima = lax.optimization_barrier(jnp.max(scores, axis=-1, keepdims=True))
        weights = jnp.exp(scores - maxima)
        denominator = lax.optimization_barrier(jnp.sum(weights, axis=-1))
        rounded = lax.optimization_barrier(weights.astype(jnp.bfloat16))
        numerator = jnp.einsum('tgqr,rgd->tgqd', rounded.astype(jnp.float32), values_wide)
        return (numerator / denominator[..., None]).astype(jnp.bfloat16)
    attended = lax.map(attend_block, blocked_queries).reshape(TEXT_TOKENS, QUERY_HEADS * HEAD_SIZE)
    projected = jnp.dot(attended, out_weight, preferred_element_type=jnp.float32)
    return (residual.astype(jnp.float32) + jnp.tanh(attn_gate[0]) * projected).astype(jnp.bfloat16)
```

```python
import functools

import jax
import jax.numpy as jnp
from jax import lax
from jax.experimental import pallas as pl
from jax.experimental.pallas import tpu as pltpu
from jax.sharding import PartitionSpec as P

HEAD_SIZE = 128
EPSILON = 1e-05
MESH = pl.DeviceIdType.MESH


def ring_columns(mesh):
    line = mesh.devices[0, :, 0]
    coords = [getattr(d, "coords", None) for d in line]
    if any(c is None for c in coords):
        return 1
    n = len(coords)

    def hops(order):
        return sum(
            sum(abs(a - b) for a, b in zip(coords[order[i]], coords[order[(i + 1) % n]]))
            for i in range(n)
        )

    straight = list(range(n))
    folded = straight[0::2] + straight[1::2][::-1]
    return 2 if hops(folded) < hops(straight) else 1


def norm(x, gain):
    return x * lax.rsqrt(jnp.mean(x * x, axis=-1, keepdims=True) + EPSILON) * gain


def kernel(
    n, folds, pairs,
    q_ref, vision_ref, key_ref, value_ref, out_w_ref, res_ref, qgain_ref, kgain_ref, gate_ref,
    out_ref,
    wk, wv, vis, ow, kbuf, vbuf, a0, a1, qs, pout, pin,
    load_sem, wsend, wrecv, xsend, xrecv, ksend, krecv, asend, arecv, psend, precv,
):
    group = lax.axis_index("groups")
    me = lax.axis_index("seq")
    head = lax.axis_index("head")
    half = n // folds

    def position(i):
        if folds == 1:
            return i
        z, y = i // 2, i % 2
        return z * (1 - y) + (n - 1 - z) * y

    def index(p):
        if folds == 1:
            return p
        y = p // half
        z = p * (1 - y) + (n - 1 - p) * y
        return z * 2 + y

    pos = position(me)

    def at(offset):
        return index(lax.rem(pos + (n + offset), n))

    neighbours = {1: at(1), -1: at(-1)}
    streams = [(1, 0, n // 2), (-1, 1, n // 2), (1, 1, n // 2 - 1), (-1, 0, n // 2 - 1)]

    def piece(view, send, recv, t, s, received):
        direction, b, _ = streams[t]
        owner = at(-direction * (s + received))
        v = view(b, owner)
        return pltpu.make_async_remote_copy(
            src_ref=v, dst_ref=v, send_sem=send.at[t, s], recv_sem=recv.at[t, s],
            device_id={"seq": neighbours[direction]}, device_id_type=MESH,
        )

    def begin(view, send, recv, b):
        for t, stream in enumerate(streams):
            if stream[1] == b and stream[2] > 0:
                piece(view, send, recv, t, 0, 0).start()

    def run(view, send, recv, arrived=None):
        for s in range(n // 2):
            for t, stream in enumerate(streams):
                if s < stream[2]:
                    piece(view, send, recv, t, s, 1).wait_recv()
                    if s + 1 < stream[2]:
                        piece(view, send, recv, t, s + 1, 0).start()
                    if arrived is not None:
                        arrived(t, s)

    def drain(view, send, recv):
        for t, stream in enumerate(streams):
            for s in range(stream[2]):
                piece(view, send, recv, t, s, 0).wait_send()

    rows = key_ref.shape[0]
    own = pl.ds(pl.multiple_of(me * rows, 16), rows)
    loads = [
        pltpu.make_async_copy(key_ref, wk.at[own], load_sem.at[0]),
        pltpu.make_async_copy(value_ref, wv.at[own], load_sem.at[1]),
        pltpu.make_async_copy(vision_ref, vis, load_sem.at[2]),
        pltpu.make_async_copy(out_w_ref, ow, load_sem.at[3]),
    ]
    for load in loads:
        load.start()

    barrier = pltpu.get_barrier_semaphore()
    for target in neighbours.values():
        pl.semaphore_signal(barrier, inc=1, device_id={"seq": target}, device_id_type=MESH)
    pl.semaphore_signal(barrier, inc=1, device_id={"head": 1 - head}, device_id_type=MESH)
    if pairs:
        odd = group % 2
        partner = group + 1 - 2 * odd
        pl.semaphore_signal(barrier, inc=1, device_id={"groups": partner}, device_id_type=MESH)
    pl.semaphore_wait(barrier, 4 if pairs else 3)

    loads[0].wait()
    loads[1].wait()

    shared = (rows * 3 // 10 + 15) // 16 * 16 if pairs else 0
    ringed = rows - shared
    weights = (wk, wv)

    def weight_view(b, owner):
        start = owner * rows
        if pairs:
            start = start + odd * shared
        return weights[b].at[pl.ds(pl.multiple_of(start, 16), ringed)]

    def cross(t, s, received):
        direction, b, _ = streams[t]
        owner = at(-direction * (s + 1))
        which = (1 - odd) if received else odd
        start = owner * rows + which * ringed
        v = weights[b].at[pl.ds(pl.multiple_of(start, 16), shared)]
        return pltpu.make_async_remote_copy(
            src_ref=v, dst_ref=v, send_sem=xsend.at[t, s], recv_sem=xrecv.at[t, s],
            device_id={"groups": partner}, device_id_type=MESH,
        )

    begin(weight_view, wsend, wrecv, 0)
    begin(weight_view, wsend, wrecv, 1)

    text = q_ref.shape[0]
    kv_local = key_ref.shape[1] // HEAD_SIZE
    heads_local = q_ref.shape[1] // HEAD_SIZE
    per_group = heads_local // kv_local
    for h in range(heads_local):
        x = q_ref[:, h * HEAD_SIZE:(h + 1) * HEAD_SIZE].astype(jnp.float32)
        qs[h * text:(h + 1) * text, :] = norm(x, qgain_ref[...]).astype(jnp.bfloat16)

    run(weight_view, wsend, wrecv, (lambda t, s: cross(t, s, False).start()) if pairs else None)
    if pairs:
        for t, stream in enumerate(streams):
            for s in range(stream[2]):
                cross(t, s, True).wait_recv()
    loads[2].wait()

    vrows, width = vis.shape
    mine = pl.ds(pl.multiple_of(me * vrows, 16), vrows)
    bufs = (kbuf, vbuf)

    def kv_view(b, owner):
        return bufs[b].at[pl.ds(pl.multiple_of(owner * vrows, 16), vrows)]

    keys = jnp.dot(vis[...], wk[...], preferred_element_type=jnp.float32)
    for g in range(kv_local):
        cols = slice(g * HEAD_SIZE, (g + 1) * HEAD_SIZE)
        kbuf[mine, cols] = norm(keys[:, cols], kgain_ref[...]).astype(jnp.bfloat16)
    begin(kv_view, ksend, krecv, 0)
    values = jnp.dot(vis[...], wv[...], preferred_element_type=jnp.float32)
    vbuf[mine, :] = values.astype(jnp.bfloat16)
    begin(kv_view, ksend, krecv, 1)
    run(kv_view, ksend, krecv)

    total = kbuf.shape[0]
    block = min(total, 2048)
    scale = HEAD_SIZE ** (-0.5)
    attended = (a0, a1)
    mine_text = pl.ds(pl.multiple_of(me * text, 16), text)

    def text_view(b, owner):
        return attended[b].at[pl.ds(pl.multiple_of(owner * text, 16), text)]

    groups_per_buffer = kv_local // 2
    for g in range(kv_local):
        cols = slice(g * HEAD_SIZE, (g + 1) * HEAD_SIZE)
        q = qs[g * per_group * text:(g + 1) * per_group * text, :]
        top = None
        for r in range(0, total, block):
            scores = lax.dot_general(
                q, kbuf[r:r + block, cols], (((1,), (1,)), ((), ())),
                preferred_element_type=jnp.float32,
            ) * scale
            high = jnp.max(scores, axis=-1, keepdims=True)
            new = high if top is None else jnp.maximum(top, high)
            weight = jnp.exp(scores - new)
            part = jnp.sum(weight, axis=-1, keepdims=True)
            product = jnp.dot(
                weight.astype(jnp.bfloat16), vbuf[r:r + block, cols],
                preferred_element_type=jnp.float32,
            )
            if top is None:
                den, num = part, product
            else:
                rescale = jnp.exp(top - new)
                den, num = den * rescale + part, num * rescale + product
            top = new
        result = (num / den).astype(jnp.bfloat16)
        b, inner = g // groups_per_buffer, g % groups_per_buffer
        for h in range(per_group):
            column = (inner * per_group + h) * HEAD_SIZE
            attended[b][mine_text, column:column + HEAD_SIZE] = result[h * text:(h + 1) * text, :]
        if inner == groups_per_buffer - 1:
            begin(text_view, asend, arecv, b)
    run(text_view, asend, arecv)
    loads[3].wait()

    out_rows = out_ref.shape[0]
    depth = a0.shape[1]

    def project(which):
        r = pl.ds(pl.multiple_of(which * out_rows, 16), out_rows)
        return jnp.dot(
            a0[r, :], ow[:depth, :], preferred_element_type=jnp.float32
        ) + jnp.dot(a1[r, :], ow[depth:, :], preferred_element_type=jnp.float32)

    pout[...] = project(1 - head).astype(jnp.bfloat16)
    swap = pltpu.make_async_remote_copy(
        src_ref=pout, dst_ref=pin, send_sem=psend, recv_sem=precv,
        device_id={"head": 1 - head}, device_id_type=MESH,
    )
    swap.start()
    projected = project(head)
    swap.wait_recv()
    out_ref[...] = (
        res_ref[...].astype(jnp.float32)
        + jnp.tanh(gate_ref[...]) * (projected + pin[...].astype(jnp.float32))
    ).astype(out_ref.dtype)

    swap.wait_send()
    drain(weight_view, wsend, wrecv)
    if pairs:
        for t, stream in enumerate(streams):
            for s in range(stream[2]):
                cross(t, s, False).wait_send()
    drain(kv_view, ksend, krecv)
    drain(text_view, asend, arecv)


def body(n, folds, pairs, queries, vision, key_matrix, value_matrix, out_weight, residual,
         query_norm_gain, key_norm_gain, attn_gate):
    rows, columns = key_matrix.shape
    vrows, width = vision.shape
    text, qcols = queries.shape
    bf16 = jnp.bfloat16
    vmem = pl.BlockSpec(memory_space=pltpu.VMEM)
    hbm = pl.BlockSpec(memory_space=pl.ANY)
    steps = pltpu.SemaphoreType.DMA((4, n // 2))
    return pl.pallas_call(
        functools.partial(kernel, n, folds, pairs),
        out_shape=jax.ShapeDtypeStruct(residual.shape, residual.dtype),
        in_specs=[vmem, hbm, hbm, hbm, hbm, vmem, vmem, vmem, vmem],
        out_specs=vmem,
        scratch_shapes=[
            pltpu.VMEM((n * rows, columns), bf16),
            pltpu.VMEM((n * rows, columns), bf16),
            pltpu.VMEM((vrows, width), bf16),
            pltpu.VMEM(out_weight.shape, bf16),
            pltpu.VMEM((n * vrows, columns), bf16),
            pltpu.VMEM((n * vrows, columns), bf16),
            pltpu.VMEM((n * text, qcols // 2), bf16),
            pltpu.VMEM((n * text, qcols // 2), bf16),
            pltpu.VMEM((text * qcols // HEAD_SIZE, HEAD_SIZE), bf16),
            pltpu.VMEM(residual.shape, bf16),
            pltpu.VMEM(residual.shape, bf16),
            pltpu.SemaphoreType.DMA((4,)),
            steps, steps, steps, steps, steps, steps, steps, steps,
            pltpu.SemaphoreType.DMA,
            pltpu.SemaphoreType.DMA,
        ],
        compiler_params=pltpu.CompilerParams(
            collective_id=0, has_side_effects=True, vmem_limit_bytes=60 * 1024 * 1024
        ),
    )(
        queries, vision, key_matrix, value_matrix, out_weight, residual,
        query_norm_gain.reshape(1, HEAD_SIZE), key_norm_gain.reshape(1, HEAD_SIZE),
        attn_gate.reshape(1, 1),
    )


def solution(mesh):
    in_specs = (
        P(("groups", "seq"), "head"),
        P(("groups", "seq"), None),
        P("seq", "head"),
        P("seq", "head"),
        P("head", "seq"),
        P(("groups", "head"), "seq"),
        P(),
        P(),
        P(),
    )
    out_specs = P(("groups", "head"), "seq")
    n = mesh.shape["seq"]
    pairs = mesh.shape["groups"] % 2 == 0
    local = functools.partial(body, n, ring_columns(mesh), pairs)
    return jax.shard_map(local, mesh=mesh, in_specs=in_specs, out_specs=out_specs, check_vma=False)
```

```python
import functools

import jax
import jax.numpy as jnp
from jax import lax
from jax.experimental import pallas as pl
from jax.experimental.pallas import tpu as pltpu
from jax.sharding import PartitionSpec as P

HEAD_SIZE = 128
EPSILON = 1e-05
MESH = pl.DeviceIdType.MESH


def ring_columns(mesh):
    line = mesh.devices[0, :, 0]
    coords = [getattr(d, "coords", None) for d in line]
    if any(c is None for c in coords):
        return 1
    n = len(coords)

    def hops(order):
        return sum(
            sum(abs(a - b) for a, b in zip(coords[order[i]], coords[order[(i + 1) % n]]))
            for i in range(n)
        )

    straight = list(range(n))
    folded = straight[0::2] + straight[1::2][::-1]
    return 2 if n % 4 == 0 and hops(folded) < hops(straight) else 1


def line_split(rows, pairs):
    shared = rows * 9 // 20 // 16 * 16 if pairs else 0
    return shared, rows - shared


def norm(x, gain):
    return x * lax.rsqrt(jnp.mean(x * x, axis=-1, keepdims=True) + EPSILON) * gain


def kernel(
    n, folds, pairs,
    q_ref, vision_ref, key_ref, value_ref, out_w_ref, res_ref, qgain_ref, kgain_ref, gate_ref,
    out_ref,
    wk, wv, vis, ow, kbuf, vbuf, a0, a1, qs, pout, pin, kown, kout, kin, vout, vin,
    load_sem, wsend, wrecv, xsend, xrecv, ksend, krecv, asend, arecv, psend, precv,
    ysend, yrecv, csend, crecv,
):
    group = lax.axis_index("groups")
    me = lax.axis_index("seq")
    head = lax.axis_index("head")
    half = n // folds

    def position(i):
        if folds == 1:
            return i
        z, y = i // 2, i % 2
        return z * (1 - y) + (n - 1 - z) * y

    def index(p):
        if folds == 1:
            return p
        y = p // half
        z = p * (1 - y) + (n - 1 - p) * y
        return z * 2 + y

    pos = position(me)

    def at(offset):
        return index(lax.rem(pos + (n + offset), n))

    neighbours = {1: at(1), -1: at(-1)}
    streams = [(1, 0, n // 2), (-1, 1, n // 2), (1, 1, n // 2 - 1), (-1, 0, n // 2 - 1)]

    def piece(view, send, recv, t, s, received):
        direction, b, _ = streams[t]
        owner = at(-direction * (s + received))
        v = view(b, owner)
        return pltpu.make_async_remote_copy(
            src_ref=v, dst_ref=v, send_sem=send.at[t, s], recv_sem=recv.at[t, s],
            device_id={"seq": neighbours[direction]}, device_id_type=MESH,
        )

    def begin(view, send, recv, b):
        for t, stream in enumerate(streams):
            if stream[1] == b and stream[2] > 0:
                piece(view, send, recv, t, 0, 0).start()

    def run(view, send, recv, arrived=None):
        for s in range(n // 2):
            for t, stream in enumerate(streams):
                if s < stream[2]:
                    piece(view, send, recv, t, s, 1).wait_recv()
                    if s + 1 < stream[2]:
                        piece(view, send, recv, t, s + 1, 0).start()
                    if arrived is not None:
                        arrived(t, s)

    def drain(view, send, recv):
        for t, stream in enumerate(streams):
            for s in range(stream[2]):
                piece(view, send, recv, t, s, 0).wait_send()

    rows = key_ref.shape[0]
    vrows, width = vision_ref.shape
    text = q_ref.shape[0]
    kv_local = key_ref.shape[1] // HEAD_SIZE
    heads_local = q_ref.shape[1] // HEAD_SIZE
    per_group = heads_local // kv_local
    odd = group % 2
    partner = group + 1 - 2 * odd
    weights = (wk, wv)
    mine = pl.ds(pl.multiple_of(me * vrows, 16), vrows)
    bufs = (kbuf, vbuf)
    barrier = pltpu.get_barrier_semaphore()

    def greet(**target):
        pl.semaphore_signal(barrier, inc=1, device_id=target, device_id_type=MESH)

    def kv_view(b, owner):
        return bufs[b].at[pl.ds(pl.multiple_of(owner * vrows, 16), vrows)]

    def queries():
        for h in range(heads_local):
            x = q_ref[:, h * HEAD_SIZE:(h + 1) * HEAD_SIZE].astype(jnp.float32)
            qs[h * text:(h + 1) * text, :] = norm(x, qgain_ref[...]).astype(jnp.bfloat16)

    def store_keys(keys):
        for g in range(kv_local):
            cols = slice(g * HEAD_SIZE, (g + 1) * HEAD_SIZE)
            kbuf[mine, cols] = norm(keys[:, cols], kgain_ref[...]).astype(jnp.bfloat16)

    def line_phase():
        nz = half
        z, y = me // 2, me % 2
        other = z * 2 + 1 - y
        padded = wk.shape[0] // nz
        lead = y * (padded - rows)
        shared, ringed = line_split(rows, pairs)
        middle = ringed - shared

        def slot(b, zz, start, size):
            at_row = pl.multiple_of(zz * padded + lead + start, 16)
            return weights[b].at[pl.ds(at_row, size)]

        parts = [(odd * ringed, shared), (shared, middle)] if pairs else [(0, rows)]
        loads = [
            pltpu.make_async_copy(key_ref, slot(0, z, 0, rows), load_sem.at[0]),
            pltpu.make_async_copy(value_ref, slot(1, z, 0, rows), load_sem.at[1]),
            pltpu.make_async_copy(out_w_ref, ow, load_sem.at[3]),
        ]
        for zz in range(nz):
            column = pl.multiple_of(zz * 2 * rows + y * (2 * rows - padded), HEAD_SIZE)
            loads.append(pltpu.make_async_copy(
                vision_ref.at[:, pl.ds(column, padded)],
                vis.at[:vrows, zz * padded:(zz + 1) * padded], load_sem.at[4 + zz],
            ))
        for load in loads:
            load.start()
        greet(seq=other)
        greet(head=1 - head)
        if pairs:
            greet(groups=partner)

        @pl.when(z > 0)
        def _():
            greet(seq=(z - 1) * 2 + y)

        @pl.when(z < nz - 1)
        def _():
            greet(seq=(z + 1) * 2 + y)

        if padded > rows:
            for zz in range(nz):
                for w in weights:
                    start = pl.multiple_of(zz * padded + (1 - y) * rows, 16)
                    w[pl.ds(start, padded - rows), :] = jnp.zeros(
                        (padded - rows, w.shape[1]), w.dtype)

        peers = (3 if pairs else 2) + (z + nz - 1) // nz + (2 * nz - 2 - z) // nz
        pl.semaphore_wait(barrier, peers)

        def hop(b, d, s, part, zz):
            start, size = parts[part]
            v = slot(b, zz, start, size)
            k = (b * 2 + (d + 1) // 2) * 2 + part
            return pltpu.make_async_remote_copy(
                src_ref=v, dst_ref=v, send_sem=wsend.at[k, s], recv_sem=wrecv.at[k, s],
                device_id={"seq": (z + d) * 2 + y}, device_id_type=MESH,
            )

        def cross(b, d, s, zz, received):
            which = (1 - odd) if received else odd
            v = slot(b, zz, which * ringed, shared)
            k = b * 2 + (d + 1) // 2
            return pltpu.make_async_remote_copy(
                src_ref=v, dst_ref=v, send_sem=xsend.at[k, s], recv_sem=xrecv.at[k, s],
                device_id={"groups": partner}, device_id_type=MESH,
            )

        def can_send(d, s):
            ahead = (z < nz - 1) if d == 1 else (z > 0)
            behind = (z >= s) if d == 1 else (z + s <= nz - 1)
            return jnp.logical_and(ahead, behind)

        def gets(d, s):
            return (z > s) if d == 1 else (z + s < nz - 1)

        half_rows = vrows // 2

        def vision_out(zz):
            r = pl.ds(pl.multiple_of(head * half_rows, 16), half_rows)
            column = pl.multiple_of(zz * 2 * rows + (1 - y) * (2 * rows - padded), HEAD_SIZE)
            to = pl.ds(pl.multiple_of(vrows + head * half_rows, 16), half_rows)
            return pltpu.make_async_remote_copy(
                src_ref=vision_ref.at[r, pl.ds(column, padded)],
                dst_ref=vis.at[to, zz * padded:(zz + 1) * padded],
                send_sem=ysend.at[zz], recv_sem=yrecv.at[zz],
                device_id={"seq": other}, device_id_type=MESH,
            )

        def vision_pass(zz, received):
            which = (1 - head) if received else head
            r = pl.ds(pl.multiple_of(vrows + which * half_rows, 16), half_rows)
            v = vis.at[r, zz * padded:(zz + 1) * padded]
            return pltpu.make_async_remote_copy(
                src_ref=v, dst_ref=v, send_sem=csend.at[zz], recv_sem=crecv.at[zz],
                device_id={"head": 1 - head}, device_id_type=MESH,
            )

        def begin_line(b):
            loads[b].wait()
            for d in (1, -1):
                @pl.when(can_send(d, 0))
                def _():
                    for part in range(len(parts)):
                        hop(b, d, 0, part, z).start()

        def step(b, s):
            for part in range(len(parts)):
                for d in (1, -1):
                    zz = z - d * (s + 1)

                    @pl.when(gets(d, s))
                    def _():
                        hop(b, d, s, part, zz).wait_recv()
                        if s + 1 < nz - 1:
                            @pl.when(can_send(d, s + 1))
                            def _():
                                hop(b, d, s + 1, part, zz).start()
                        if part == 0 and pairs:
                            cross(b, d, s, zz, False).start()

        def finish(b):
            if pairs:
                for s in range(nz - 1):
                    for d in (1, -1):
                        @pl.when(gets(d, s))
                        def _():
                            cross(b, d, s, z - d * (s + 1), True).wait_recv()

        def give(b):
            src, dst = ((kout, kin), (vout, vin))[b]
            return pltpu.make_async_remote_copy(
                src_ref=src, dst_ref=dst, send_sem=ysend.at[nz + b], recv_sem=yrecv.at[nz + b],
                device_id={"seq": other}, device_id_type=MESH,
            )

        def product(b, first):
            r = slice(0, vrows) if first else slice(vrows, 2 * vrows)
            return jnp.dot(vis[r, :], weights[b][...], preferred_element_type=jnp.float32)

        begin_line(0)
        for zz in range(nz):
            vision_out(zz).start()
        queries()
        for s in range(nz - 1):
            step(0, s)
        begin_line(1)
        finish(0)
        for s in range(nz - 1):
            if s == nz - 2:
                for load in loads[3:]:
                    load.wait()
                for zz in range(nz):
                    vision_out(zz).wait_recv()
                    vision_pass(zz, False).start()
                for zz in range(nz):
                    vision_pass(zz, True).wait_recv()
                kout[...] = product(0, False)
                give(0).start()
                kown[...] = product(0, True)
            step(1, s)
        give(0).wait_recv()
        store_keys(kown[...] + kin[...])
        begin(kv_view, ksend, krecv, 0)
        finish(1)
        vout[...] = product(1, False).astype(vout.dtype)
        give(1).start()
        values = product(1, True)
        give(1).wait_recv()
        vbuf[mine, :] = (values + vin[...].astype(jnp.float32)).astype(jnp.bfloat16)
        begin(kv_view, ksend, krecv, 1)

        def settle():
            for b in range(2):
                give(b).wait_send()
                for s in range(nz - 1):
                    for d in (1, -1):
                        @pl.when(can_send(d, s))
                        def _():
                            for part in range(len(parts)):
                                hop(b, d, s, part, z - d * s).wait_send()

                        if pairs:
                            @pl.when(gets(d, s))
                            def _():
                                cross(b, d, s, z - d * (s + 1), False).wait_send()
            for zz in range(nz):
                vision_out(zz).wait_send()
                vision_pass(zz, False).wait_send()

        return loads[2], settle

    def ring_phase():
        own = pl.ds(pl.multiple_of(me * rows, 16), rows)
        loads = [
            pltpu.make_async_copy(key_ref, wk.at[own], load_sem.at[0]),
            pltpu.make_async_copy(value_ref, wv.at[own], load_sem.at[1]),
            pltpu.make_async_copy(vision_ref, vis, load_sem.at[2]),
            pltpu.make_async_copy(out_w_ref, ow, load_sem.at[3]),
        ]
        for load in loads:
            load.start()
        for target in neighbours.values():
            greet(seq=target)
        greet(head=1 - head)
        if pairs:
            greet(groups=partner)
        pl.semaphore_wait(barrier, 4 if pairs else 3)
        loads[0].wait()
        loads[1].wait()
        shared = (rows * 3 // 10 + 15) // 16 * 16 if pairs else 0
        ringed = rows - shared

        def weight_view(b, owner):
            start = owner * rows
            if pairs:
                start = start + odd * shared
            return weights[b].at[pl.ds(pl.multiple_of(start, 16), ringed)]

        def cross(t, s, received):
            direction, b, _ = streams[t]
            owner = at(-direction * (s + 1))
            which = (1 - odd) if received else odd
            start = owner * rows + which * ringed
            v = weights[b].at[pl.ds(pl.multiple_of(start, 16), shared)]
            return pltpu.make_async_remote_copy(
                src_ref=v, dst_ref=v, send_sem=xsend.at[t, s], recv_sem=xrecv.at[t, s],
                device_id={"groups": partner}, device_id_type=MESH,
            )

        begin(weight_view, wsend, wrecv, 0)
        begin(weight_view, wsend, wrecv, 1)
        queries()
        run(weight_view, wsend, wrecv,
            (lambda t, s: cross(t, s, False).start()) if pairs else None)
        if pairs:
            for t, stream in enumerate(streams):
                for s in range(stream[2]):
                    cross(t, s, True).wait_recv()
        loads[2].wait()
        store_keys(jnp.dot(vis[...], wk[...], preferred_element_type=jnp.float32))
        begin(kv_view, ksend, krecv, 0)
        values = jnp.dot(vis[...], wv[...], preferred_element_type=jnp.float32)
        vbuf[mine, :] = values.astype(jnp.bfloat16)
        begin(kv_view, ksend, krecv, 1)

        def settle():
            drain(weight_view, wsend, wrecv)
            if pairs:
                for t, stream in enumerate(streams):
                    for s in range(stream[2]):
                        cross(t, s, False).wait_send()

        return loads[3], settle

    out_load, settle = (line_phase if folds == 2 else ring_phase)()
    run(kv_view, ksend, krecv)

    total = kbuf.shape[0]
    block = min(total, 2048)
    scale = HEAD_SIZE ** (-0.5)
    attended = (a0, a1)
    mine_text = pl.ds(pl.multiple_of(me * text, 16), text)

    def text_view(b, owner):
        return attended[b].at[pl.ds(pl.multiple_of(owner * text, 16), text)]

    groups_per_buffer = kv_local // 2
    for g in range(kv_local):
        cols = slice(g * HEAD_SIZE, (g + 1) * HEAD_SIZE)
        q = qs[g * per_group * text:(g + 1) * per_group * text, :]
        top = None
        for r in range(0, total, block):
            scores = lax.dot_general(
                q, kbuf[r:r + block, cols], (((1,), (1,)), ((), ())),
                preferred_element_type=jnp.float32,
            ) * scale
            high = jnp.max(scores, axis=-1, keepdims=True)
            new = high if top is None else jnp.maximum(top, high)
            weight = jnp.exp(scores - new)
            part = jnp.sum(weight, axis=-1, keepdims=True)
            product = jnp.dot(
                weight.astype(jnp.bfloat16), vbuf[r:r + block, cols],
                preferred_element_type=jnp.float32,
            )
            if top is None:
                den, num = part, product
            else:
                rescale = jnp.exp(top - new)
                den, num = den * rescale + part, num * rescale + product
            top = new
        result = (num / den).astype(jnp.bfloat16)
        b, inner = g // groups_per_buffer, g % groups_per_buffer
        for h in range(per_group):
            column = (inner * per_group + h) * HEAD_SIZE
            attended[b][mine_text, column:column + HEAD_SIZE] = result[h * text:(h + 1) * text, :]
        if inner == groups_per_buffer - 1:
            begin(text_view, asend, arecv, b)
    run(text_view, asend, arecv)
    out_load.wait()

    out_rows = out_ref.shape[0]
    depth = a0.shape[1]

    def project(which):
        r = pl.ds(pl.multiple_of(which * out_rows, 16), out_rows)
        return jnp.dot(
            a0[r, :], ow[:depth, :], preferred_element_type=jnp.float32
        ) + jnp.dot(a1[r, :], ow[depth:, :], preferred_element_type=jnp.float32)

    pout[...] = project(1 - head).astype(jnp.bfloat16)
    swap = pltpu.make_async_remote_copy(
        src_ref=pout, dst_ref=pin, send_sem=psend, recv_sem=precv,
        device_id={"head": 1 - head}, device_id_type=MESH,
    )
    swap.start()
    projected = project(head)
    swap.wait_recv()
    out_ref[...] = (
        res_ref[...].astype(jnp.float32)
        + jnp.tanh(gate_ref[...]) * (projected + pin[...].astype(jnp.float32))
    ).astype(out_ref.dtype)

    swap.wait_send()
    settle()
    drain(kv_view, ksend, krecv)
    drain(text_view, asend, arecv)


def body(n, folds, pairs, queries, vision, key_matrix, value_matrix, out_weight, residual,
         query_norm_gain, key_norm_gain, attn_gate):
    rows, columns = key_matrix.shape
    vrows, width = vision.shape
    text, qcols = queries.shape
    bf16 = jnp.bfloat16
    vmem = pl.BlockSpec(memory_space=pltpu.VMEM)
    hbm = pl.BlockSpec(memory_space=pl.ANY)
    steps = pltpu.SemaphoreType.DMA((4, n // 2))
    hops = pltpu.SemaphoreType.DMA((8, n // 2))
    if folds == 2:
        depth = n // 2 * (-(-rows // HEAD_SIZE) * HEAD_SIZE)
        seen = (2 * vrows, depth)
        part = (vrows, columns)
    else:
        depth = n * rows
        seen = (vrows, width)
        part = (16, HEAD_SIZE)
    return pl.pallas_call(
        functools.partial(kernel, n, folds, pairs),
        out_shape=jax.ShapeDtypeStruct(residual.shape, residual.dtype),
        in_specs=[vmem, hbm, hbm, hbm, hbm, vmem, vmem, vmem, vmem],
        out_specs=vmem,
        scratch_shapes=[
            pltpu.VMEM((depth, columns), bf16),
            pltpu.VMEM((depth, columns), bf16),
            pltpu.VMEM(seen, bf16),
            pltpu.VMEM(out_weight.shape, bf16),
            pltpu.VMEM((n * vrows, columns), bf16),
            pltpu.VMEM((n * vrows, columns), bf16),
            pltpu.VMEM((n * text, qcols // 2), bf16),
            pltpu.VMEM((n * text, qcols // 2), bf16),
            pltpu.VMEM((text * qcols // HEAD_SIZE, HEAD_SIZE), bf16),
            pltpu.VMEM(residual.shape, bf16),
            pltpu.VMEM(residual.shape, bf16),
            pltpu.VMEM(part, jnp.float32),
            pltpu.VMEM(part, jnp.float32),
            pltpu.VMEM(part, jnp.float32),
            pltpu.VMEM(part, bf16),
            pltpu.VMEM(part, bf16),
            pltpu.SemaphoreType.DMA((4 + n // 2,)),
            hops, hops, steps, steps, steps, steps, steps, steps,
            pltpu.SemaphoreType.DMA,
            pltpu.SemaphoreType.DMA,
            pltpu.SemaphoreType.DMA((n // 2 + 2,)),
            pltpu.SemaphoreType.DMA((n // 2 + 2,)),
            pltpu.SemaphoreType.DMA((n // 2,)),
            pltpu.SemaphoreType.DMA((n // 2,)),
        ],
        compiler_params=pltpu.CompilerParams(
            collective_id=0, has_side_effects=True, vmem_limit_bytes=60 * 1024 * 1024
        ),
    )(
        queries, vision, key_matrix, value_matrix, out_weight, residual,
        query_norm_gain.reshape(1, HEAD_SIZE), key_norm_gain.reshape(1, HEAD_SIZE),
        attn_gate.reshape(1, 1),
    )


def solution(mesh):
    in_specs = (
        P(("groups", "seq"), "head"),
        P(("groups", "seq"), None),
        P("seq", "head"),
        P("seq", "head"),
        P("head", "seq"),
        P(("groups", "head"), "seq"),
        P(),
        P(),
        P(),
    )
    out_specs = P(("groups", "head"), "seq")
    n = mesh.shape["seq"]
    pairs = mesh.shape["groups"] % 2 == 0
    local = functools.partial(body, n, ring_columns(mesh), pairs)
    return jax.shard_map(local, mesh=mesh, in_specs=in_specs, out_specs=out_specs, check_vma=False)
```

```python
import functools

import jax
import jax.numpy as jnp
from jax import lax
from jax.experimental import pallas as pl
from jax.experimental.pallas import tpu as pltpu
from jax.sharding import PartitionSpec as P

HEAD_SIZE = 128
EPSILON = 1e-05
MESH = pl.DeviceIdType.MESH


def ring_columns(mesh):
    line = mesh.devices[0, :, 0]
    coords = [getattr(d, "coords", None) for d in line]
    if any(c is None for c in coords):
        return 1
    n = len(coords)

    def hops(order):
        return sum(
            sum(abs(a - b) for a, b in zip(coords[order[i]], coords[order[(i + 1) % n]]))
            for i in range(n)
        )

    straight = list(range(n))
    folded = straight[0::2] + straight[1::2][::-1]
    return 2 if n % 4 == 0 and hops(folded) < hops(straight) else 1


def line_split(rows, pairs):
    shared = rows * 19 // 40 // 16 * 16 if pairs else 0
    return shared, rows - shared


def norm(x, gain):
    return x * lax.rsqrt(jnp.mean(x * x, axis=-1, keepdims=True) + EPSILON) * gain


def kernel(
    n, folds, pairs,
    q_ref, vision_ref, key_ref, value_ref, out_w_ref, res_ref, qgain_ref, kgain_ref, gate_ref,
    out_ref,
    wk, wv, vis, ow, kbuf, vbuf, a0, a1, qs, pout, pin, kown, kout, kin, vout, vin,
    load_sem, wsend, wrecv, xsend, xrecv, ksend, krecv, asend, arecv, psend, precv,
    ysend, yrecv, csend, crecv,
):
    group = lax.axis_index("groups")
    me = lax.axis_index("seq")
    head = lax.axis_index("head")
    half = n // folds

    def position(i):
        if folds == 1:
            return i
        z, y = i // 2, i % 2
        return z * (1 - y) + (n - 1 - z) * y

    def index(p):
        if folds == 1:
            return p
        y = p // half
        z = p * (1 - y) + (n - 1 - p) * y
        return z * 2 + y

    pos = position(me)

    def at(offset):
        return index(lax.rem(pos + (n + offset), n))

    neighbours = {1: at(1), -1: at(-1)}
    streams = [(1, 0, n // 2), (-1, 1, n // 2), (1, 1, n // 2 - 1), (-1, 0, n // 2 - 1)]

    def piece(view, send, recv, t, s, received):
        direction, b, _ = streams[t]
        owner = at(-direction * (s + received))
        v = view(b, owner)
        return pltpu.make_async_remote_copy(
            src_ref=v, dst_ref=v, send_sem=send.at[t, s], recv_sem=recv.at[t, s],
            device_id={"seq": neighbours[direction]}, device_id_type=MESH,
        )

    def begin(view, send, recv, b):
        for t, stream in enumerate(streams):
            if stream[1] == b and stream[2] > 0:
                piece(view, send, recv, t, 0, 0).start()

    def run(view, send, recv, arrived=None):
        for s in range(n // 2):
            for t, stream in enumerate(streams):
                if s < stream[2]:
                    piece(view, send, recv, t, s, 1).wait_recv()
                    if s + 1 < stream[2]:
                        piece(view, send, recv, t, s + 1, 0).start()
                    if arrived is not None:
                        arrived(t, s)

    def drain(view, send, recv):
        for t, stream in enumerate(streams):
            for s in range(stream[2]):
                piece(view, send, recv, t, s, 0).wait_send()

    rows = key_ref.shape[0]
    vrows, width = vision_ref.shape
    text = q_ref.shape[0]
    kv_local = key_ref.shape[1] // HEAD_SIZE
    heads_local = q_ref.shape[1] // HEAD_SIZE
    per_group = heads_local // kv_local
    odd = group % 2
    partner = group + 1 - 2 * odd
    weights = (wk, wv)
    mine = pl.ds(pl.multiple_of(me * vrows, 16), vrows)
    bufs = (kbuf, vbuf)
    barrier = pltpu.get_barrier_semaphore()

    def greet(**target):
        pl.semaphore_signal(barrier, inc=1, device_id=target, device_id_type=MESH)

    def kv_view(b, owner):
        return bufs[b].at[pl.ds(pl.multiple_of(owner * vrows, 16), vrows)]

    def queries():
        for h in range(heads_local):
            x = q_ref[:, h * HEAD_SIZE:(h + 1) * HEAD_SIZE].astype(jnp.float32)
            qs[h * text:(h + 1) * text, :] = norm(x, qgain_ref[...]).astype(jnp.bfloat16)

    def store_keys(keys):
        for g in range(kv_local):
            cols = slice(g * HEAD_SIZE, (g + 1) * HEAD_SIZE)
            kbuf[mine, cols] = norm(keys[:, cols], kgain_ref[...]).astype(jnp.bfloat16)

    def line_phase():
        nz = half
        z, y = me // 2, me % 2
        other = z * 2 + 1 - y
        padded = wk.shape[0] // nz
        lead = y * (padded - rows)
        shared, ringed = line_split(rows, pairs)
        middle = ringed - shared

        def slot(b, zz, start, size):
            at_row = pl.multiple_of(zz * padded + lead + start, 16)
            return weights[b].at[pl.ds(at_row, size)]

        parts = [(odd * ringed, shared), (shared, middle)] if pairs else [(0, rows)]
        loads = [
            pltpu.make_async_copy(key_ref, slot(0, z, 0, rows), load_sem.at[0]),
            pltpu.make_async_copy(value_ref, slot(1, z, 0, rows), load_sem.at[1]),
            pltpu.make_async_copy(out_w_ref, ow, load_sem.at[3]),
        ]
        for zz in range(nz):
            column = pl.multiple_of(zz * 2 * rows + y * (2 * rows - padded), HEAD_SIZE)
            loads.append(pltpu.make_async_copy(
                vision_ref.at[:, pl.ds(column, padded)],
                vis.at[:vrows, zz * padded:(zz + 1) * padded], load_sem.at[4 + zz],
            ))
        loads[0].start()
        loads[1].start()
        greet(seq=other)
        greet(head=1 - head)
        if pairs:
            greet(groups=partner)

        @pl.when(z > 0)
        def _():
            greet(seq=(z - 1) * 2 + y)

        @pl.when(z < nz - 1)
        def _():
            greet(seq=(z + 1) * 2 + y)

        if padded > rows:
            for zz in range(nz):
                for w in weights:
                    start = pl.multiple_of(zz * padded + (1 - y) * rows, 16)
                    w[pl.ds(start, padded - rows), :] = jnp.zeros(
                        (padded - rows, w.shape[1]), w.dtype)

        peers = (3 if pairs else 2) + (z + nz - 1) // nz + (2 * nz - 2 - z) // nz
        pl.semaphore_wait(barrier, peers)

        def hop(b, d, s, part, zz):
            start, size = parts[part]
            v = slot(b, zz, start, size)
            k = (b * 2 + (d + 1) // 2) * 2 + part
            return pltpu.make_async_remote_copy(
                src_ref=v, dst_ref=v, send_sem=wsend.at[k, s], recv_sem=wrecv.at[k, s],
                device_id={"seq": (z + d) * 2 + y}, device_id_type=MESH,
            )

        def cross(b, d, s, zz, received):
            which = (1 - odd) if received else odd
            v = slot(b, zz, which * ringed, shared)
            k = b * 2 + (d + 1) // 2
            return pltpu.make_async_remote_copy(
                src_ref=v, dst_ref=v, send_sem=xsend.at[k, s], recv_sem=xrecv.at[k, s],
                device_id={"groups": partner}, device_id_type=MESH,
            )

        def can_send(d, s):
            ahead = (z < nz - 1) if d == 1 else (z > 0)
            behind = (z >= s) if d == 1 else (z + s <= nz - 1)
            return jnp.logical_and(ahead, behind)

        def gets(d, s):
            return (z > s) if d == 1 else (z + s < nz - 1)

        half_rows = vrows // 2

        def vision_out(zz):
            r = pl.ds(pl.multiple_of(head * half_rows, 16), half_rows)
            column = pl.multiple_of(zz * 2 * rows + (1 - y) * (2 * rows - padded), HEAD_SIZE)
            to = pl.ds(pl.multiple_of(vrows + head * half_rows, 16), half_rows)
            return pltpu.make_async_remote_copy(
                src_ref=vision_ref.at[r, pl.ds(column, padded)],
                dst_ref=vis.at[to, zz * padded:(zz + 1) * padded],
                send_sem=ysend.at[zz], recv_sem=yrecv.at[zz],
                device_id={"seq": other}, device_id_type=MESH,
            )

        def vision_pass(zz, received):
            which = (1 - head) if received else head
            r = pl.ds(pl.multiple_of(vrows + which * half_rows, 16), half_rows)
            v = vis.at[r, zz * padded:(zz + 1) * padded]
            return pltpu.make_async_remote_copy(
                src_ref=v, dst_ref=v, send_sem=csend.at[zz], recv_sem=crecv.at[zz],
                device_id={"head": 1 - head}, device_id_type=MESH,
            )

        def begin_line(b):
            loads[b].wait()
            for d in (1, -1):
                @pl.when(can_send(d, 0))
                def _():
                    for part in range(len(parts)):
                        hop(b, d, 0, part, z).start()

        def step(b, s):
            for part in range(len(parts)):
                for d in (1, -1):
                    zz = z - d * (s + 1)

                    @pl.when(gets(d, s))
                    def _():
                        hop(b, d, s, part, zz).wait_recv()
                        if s + 1 < nz - 1:
                            @pl.when(can_send(d, s + 1))
                            def _():
                                hop(b, d, s + 1, part, zz).start()
                        if part == 0 and pairs:
                            cross(b, d, s, zz, False).start()

        def finish(b):
            if pairs:
                for s in range(nz - 1):
                    for d in (1, -1):
                        @pl.when(gets(d, s))
                        def _():
                            cross(b, d, s, z - d * (s + 1), True).wait_recv()

        def give(b):
            src, dst = ((kout, kin), (vout, vin))[b]
            return pltpu.make_async_remote_copy(
                src_ref=src, dst_ref=dst, send_sem=ysend.at[nz + b], recv_sem=yrecv.at[nz + b],
                device_id={"seq": other}, device_id_type=MESH,
            )

        def product(b, first):
            r = slice(0, vrows) if first else slice(vrows, 2 * vrows)
            return jnp.dot(vis[r, :], weights[b][...], preferred_element_type=jnp.float32)

        begin_line(0)
        for zz in range(nz):
            vision_out(zz).start()
        for load in loads[2:]:
            load.start()
        queries()
        for s in range(nz - 1):
            step(0, s)
        begin_line(1)
        finish(0)
        for s in range(nz - 1):
            if s == nz - 2:
                for load in loads[3:]:
                    load.wait()
                for zz in range(nz):
                    vision_out(zz).wait_recv()
                    vision_pass(zz, False).start()
                for zz in range(nz):
                    vision_pass(zz, True).wait_recv()
                kout[...] = product(0, False)
                give(0).start()
                kown[...] = product(0, True)
            step(1, s)
        give(0).wait_recv()
        store_keys(kown[...] + kin[...])
        begin(kv_view, ksend, krecv, 0)
        finish(1)
        vout[...] = product(1, False).astype(vout.dtype)
        give(1).start()
        values = product(1, True)
        give(1).wait_recv()
        vbuf[mine, :] = (values + vin[...].astype(jnp.float32)).astype(jnp.bfloat16)
        begin(kv_view, ksend, krecv, 1)

        def settle():
            for b in range(2):
                give(b).wait_send()
                for s in range(nz - 1):
                    for d in (1, -1):
                        @pl.when(can_send(d, s))
                        def _():
                            for part in range(len(parts)):
                                hop(b, d, s, part, z - d * s).wait_send()

                        if pairs:
                            @pl.when(gets(d, s))
                            def _():
                                cross(b, d, s, z - d * (s + 1), False).wait_send()
            for zz in range(nz):
                vision_out(zz).wait_send()
                vision_pass(zz, False).wait_send()

        return loads[2], settle

    def ring_phase():
        own = pl.ds(pl.multiple_of(me * rows, 16), rows)
        loads = [
            pltpu.make_async_copy(key_ref, wk.at[own], load_sem.at[0]),
            pltpu.make_async_copy(value_ref, wv.at[own], load_sem.at[1]),
            pltpu.make_async_copy(vision_ref, vis, load_sem.at[2]),
            pltpu.make_async_copy(out_w_ref, ow, load_sem.at[3]),
        ]
        for load in loads:
            load.start()
        for target in neighbours.values():
            greet(seq=target)
        greet(head=1 - head)
        if pairs:
            greet(groups=partner)
        pl.semaphore_wait(barrier, 4 if pairs else 3)
        loads[0].wait()
        loads[1].wait()
        shared = (rows * 3 // 10 + 15) // 16 * 16 if pairs else 0
        ringed = rows - shared

        def weight_view(b, owner):
            start = owner * rows
            if pairs:
                start = start + odd * shared
            return weights[b].at[pl.ds(pl.multiple_of(start, 16), ringed)]

        def cross(t, s, received):
            direction, b, _ = streams[t]
            owner = at(-direction * (s + 1))
            which = (1 - odd) if received else odd
            start = owner * rows + which * ringed
            v = weights[b].at[pl.ds(pl.multiple_of(start, 16), shared)]
            return pltpu.make_async_remote_copy(
                src_ref=v, dst_ref=v, send_sem=xsend.at[t, s], recv_sem=xrecv.at[t, s],
                device_id={"groups": partner}, device_id_type=MESH,
            )

        begin(weight_view, wsend, wrecv, 0)
        begin(weight_view, wsend, wrecv, 1)
        queries()
        run(weight_view, wsend, wrecv,
            (lambda t, s: cross(t, s, False).start()) if pairs else None)
        if pairs:
            for t, stream in enumerate(streams):
                for s in range(stream[2]):
                    cross(t, s, True).wait_recv()
        loads[2].wait()
        store_keys(jnp.dot(vis[...], wk[...], preferred_element_type=jnp.float32))
        begin(kv_view, ksend, krecv, 0)
        values = jnp.dot(vis[...], wv[...], preferred_element_type=jnp.float32)
        vbuf[mine, :] = values.astype(jnp.bfloat16)
        begin(kv_view, ksend, krecv, 1)

        def settle():
            drain(weight_view, wsend, wrecv)
            if pairs:
                for t, stream in enumerate(streams):
                    for s in range(stream[2]):
                        cross(t, s, False).wait_send()

        return loads[3], settle

    out_load, settle = (line_phase if folds == 2 else ring_phase)()
    run(kv_view, ksend, krecv)

    total = kbuf.shape[0]
    block = min(total, 2048)
    scale = HEAD_SIZE ** (-0.5)
    attended = (a0, a1)
    mine_text = pl.ds(pl.multiple_of(me * text, 16), text)

    def text_view(b, owner):
        return attended[b].at[pl.ds(pl.multiple_of(owner * text, 16), text)]

    groups_per_buffer = kv_local // 2
    for g in range(kv_local):
        cols = slice(g * HEAD_SIZE, (g + 1) * HEAD_SIZE)
        q = qs[g * per_group * text:(g + 1) * per_group * text, :]
        top = None
        for r in range(0, total, block):
            scores = lax.dot_general(
                q, kbuf[r:r + block, cols], (((1,), (1,)), ((), ())),
                preferred_element_type=jnp.float32,
            ) * scale
            high = jnp.max(scores, axis=-1, keepdims=True)
            new = high if top is None else jnp.maximum(top, high)
            weight = jnp.exp(scores - new)
            part = jnp.sum(weight, axis=-1, keepdims=True)
            product = jnp.dot(
                weight.astype(jnp.bfloat16), vbuf[r:r + block, cols],
                preferred_element_type=jnp.float32,
            )
            if top is None:
                den, num = part, product
            else:
                rescale = jnp.exp(top - new)
                den, num = den * rescale + part, num * rescale + product
            top = new
        result = (num / den).astype(jnp.bfloat16)
        b, inner = g // groups_per_buffer, g % groups_per_buffer
        for h in range(per_group):
            column = (inner * per_group + h) * HEAD_SIZE
            attended[b][mine_text, column:column + HEAD_SIZE] = result[h * text:(h + 1) * text, :]
        if inner == groups_per_buffer - 1:
            begin(text_view, asend, arecv, b)
    run(text_view, asend, arecv)
    out_load.wait()

    out_rows = out_ref.shape[0]
    depth = a0.shape[1]

    def project(which):
        r = pl.ds(pl.multiple_of(which * out_rows, 16), out_rows)
        return jnp.dot(
            a0[r, :], ow[:depth, :], preferred_element_type=jnp.float32
        ) + jnp.dot(a1[r, :], ow[depth:, :], preferred_element_type=jnp.float32)

    pout[...] = project(1 - head).astype(jnp.bfloat16)
    swap = pltpu.make_async_remote_copy(
        src_ref=pout, dst_ref=pin, send_sem=psend, recv_sem=precv,
        device_id={"head": 1 - head}, device_id_type=MESH,
    )
    swap.start()
    projected = project(head)
    swap.wait_recv()
    out_ref[...] = (
        res_ref[...].astype(jnp.float32)
        + jnp.tanh(gate_ref[...]) * (projected + pin[...].astype(jnp.float32))
    ).astype(out_ref.dtype)

    swap.wait_send()
    settle()
    drain(kv_view, ksend, krecv)
    drain(text_view, asend, arecv)


def body(n, folds, pairs, queries, vision, key_matrix, value_matrix, out_weight, residual,
         query_norm_gain, key_norm_gain, attn_gate):
    rows, columns = key_matrix.shape
    vrows, width = vision.shape
    text, qcols = queries.shape
    bf16 = jnp.bfloat16
    vmem = pl.BlockSpec(memory_space=pltpu.VMEM)
    hbm = pl.BlockSpec(memory_space=pl.ANY)
    steps = pltpu.SemaphoreType.DMA((4, n // 2))
    hops = pltpu.SemaphoreType.DMA((8, n // 2))
    if folds == 2:
        depth = n // 2 * (-(-rows // HEAD_SIZE) * HEAD_SIZE)
        seen = (2 * vrows, depth)
        part = (vrows, columns)
    else:
        depth = n * rows
        seen = (vrows, width)
        part = (16, HEAD_SIZE)
    return pl.pallas_call(
        functools.partial(kernel, n, folds, pairs),
        out_shape=jax.ShapeDtypeStruct(residual.shape, residual.dtype),
        in_specs=[vmem, hbm, hbm, hbm, hbm, vmem, vmem, vmem, vmem],
        out_specs=vmem,
        scratch_shapes=[
            pltpu.VMEM((depth, columns), bf16),
            pltpu.VMEM((depth, columns), bf16),
            pltpu.VMEM(seen, bf16),
            pltpu.VMEM(out_weight.shape, bf16),
            pltpu.VMEM((n * vrows, columns), bf16),
            pltpu.VMEM((n * vrows, columns), bf16),
            pltpu.VMEM((n * text, qcols // 2), bf16),
            pltpu.VMEM((n * text, qcols // 2), bf16),
            pltpu.VMEM((text * qcols // HEAD_SIZE, HEAD_SIZE), bf16),
            pltpu.VMEM(residual.shape, bf16),
            pltpu.VMEM(residual.shape, bf16),
            pltpu.VMEM(part, jnp.float32),
            pltpu.VMEM(part, jnp.float32),
            pltpu.VMEM(part, jnp.float32),
            pltpu.VMEM(part, bf16),
            pltpu.VMEM(part, bf16),
            pltpu.SemaphoreType.DMA((4 + n // 2,)),
            hops, hops, steps, steps, steps, steps, steps, steps,
            pltpu.SemaphoreType.DMA,
            pltpu.SemaphoreType.DMA,
            pltpu.SemaphoreType.DMA((n // 2 + 2,)),
            pltpu.SemaphoreType.DMA((n // 2 + 2,)),
            pltpu.SemaphoreType.DMA((n // 2,)),
            pltpu.SemaphoreType.DMA((n // 2,)),
        ],
        compiler_params=pltpu.CompilerParams(
            collective_id=0, has_side_effects=True, vmem_limit_bytes=60 * 1024 * 1024
        ),
    )(
        queries, vision, key_matrix, value_matrix, out_weight, residual,
        query_norm_gain.reshape(1, HEAD_SIZE), key_norm_gain.reshape(1, HEAD_SIZE),
        attn_gate.reshape(1, 1),
    )


def solution(mesh):
    in_specs = (
        P(("groups", "seq"), "head"),
        P(("groups", "seq"), None),
        P("seq", "head"),
        P("seq", "head"),
        P("head", "seq"),
        P(("groups", "head"), "seq"),
        P(),
        P(),
        P(),
    )
    out_specs = P(("groups", "head"), "seq")
    n = mesh.shape["seq"]
    pairs = mesh.shape["groups"] % 2 == 0
    local = functools.partial(body, n, ring_columns(mesh), pairs)
    return jax.shard_map(local, mesh=mesh, in_specs=in_specs, out_specs=out_specs, check_vma=False)
```
